32 devices in a mesh: wide: 8 (over y, x, core), narrow: 4 (over z).
Axes of the slice: x: 2, y: 2, z: 4, core: 2. Of those that a mesh axis runs over, the one named last changes fastest.
Arguments:
- sources: bfloat16 [2, 1024, 8192], P(None, None, ('wide', 'narrow')), may hold values from -6 to 6
- leaf_in: bfloat16 [2, 128, 64, 64], P(None, ('wide', 'narrow')), may hold values from -0.75 to 0.75
- transfer: bfloat16 [7, 2, 128, 64, 128], P(None, None, ('wide', 'narrow')), may hold values from -0.5 to 0.5
- leaf_out: bfloat16 [2, 128, 64, 64], P(None, ('wide', 'narrow')), may hold values from -0.75 to 0.75
Outputs:
- targets: bfloat16 [2, 1024, 8192], P(None, None, ('wide', 'narrow'))
The draws below stay inside these ranges and needn't reach their ends.
All inputs are finite; a program needn't handle non-finite values.
Results may differ from the reference program's by a relative error of at most 0.0095.
Values may be sent and summed in bfloat16 or wider, within the bound.
A program may use at most 64 MiB of HBM per device.

```python
import jax
import jax.numpy as jnp

RANK = 64
LEAF = 64
RHS = 1024
LEVELS = 7
BLOCKS = 128
POINTS = 8192


def levels(key, extent, pieces, low, top_value):
    def one(dim, shards_of):
        heights = jax.random.uniform(jax.random.fold_in(jax.random.fold_in(key, 6), dim), (shards_of,), jnp.float32, low / len(pieces), top_value / len(pieces))
        return jnp.repeat(jnp.exp(heights), extent[dim] // shards_of).reshape((-1,) + (1,) * (len(extent) - dim - 1))

    gain = one(*pieces[0])
    for cut in pieces[1:]:
        gain = gain * one(*cut)
    return gain


def centred(rng, extent, spread, reach, cuts=(), kind=jnp.bfloat16):
    entries = spread * jax.random.normal(rng, extent, jnp.float32)
    if cuts:
        entries = entries * levels(rng, extent, cuts, -0.22, 0.18)
    return jnp.clip(entries, -reach, reach).astype(kind)


def setup_inputs(seed: int = 0) -> dict:
    key_of = jax.random.split(jax.random.key(seed), 5)
    return {
        "sources": centred(key_of[0], (2, RHS, POINTS), 1.0, 6.0, ((2, 32),)),
        "leaf_in": centred(key_of[1], (2, BLOCKS, LEAF, RANK), LEAF ** -0.5, 0.75, ((1, 32),)),
        "transfer": centred(key_of[2], (LEVELS, 2, BLOCKS, RANK, 2 * RANK), (2 * RANK) ** -0.5, 0.5, ((2, 32),)),
        "leaf_out": centred(key_of[3], (2, BLOCKS, RANK, LEAF), RANK ** -0.5, 0.75, ((1, 32),)),
    }


def level_apply(coef, weight, bit):
    rows, blocks, rank = coef.shape
    grouped = coef.reshape(rows, blocks // (2 * 2 ** bit), 2, 2 ** bit, rank)
    partner = grouped[:, :, ::-1].reshape(rows, blocks, rank)
    joined = jnp.concatenate([coef, partner], axis=-1).astype(jnp.float32)
    mixed = jnp.einsum('akj,koj->ako', joined, weight.astype(jnp.float32))
    return mixed.astype(jnp.bfloat16)


def reference(sources, leaf_in, transfer, leaf_out):
    results = []
    for half in range(2):
        points_in = sources[1 - half].reshape(RHS, BLOCKS, LEAF).astype(jnp.float32)
        coef = jnp.einsum('akm,kmr->akr', points_in, leaf_in[half].astype(jnp.float32)).astype(jnp.bfloat16)
        for level in range(LEVELS):
            coef = level_apply(coef, transfer[level, half], level)
        images = jnp.einsum('akr,krm->akm', coef.astype(jnp.float32), leaf_out[half].astype(jnp.float32))
        results.append(images.astype(jnp.bfloat16).reshape(RHS, BLOCKS * LEAF))
    return jnp.stack(results)
```

```python
import functools

import jax
import jax.numpy as jnp
from jax import lax
from jax.experimental import pallas as pl
from jax.experimental.pallas import tpu as pltpu
from jax.sharding import PartitionSpec as P

MESH = pl.DeviceIdType.MESH
CHUNK_ROWS = 128
FIRST_GAPS = (2, 2)
GAP = 1


def dot_nt(x, w):
    return lax.dot_general(x, w, (((1,), (1,)), ((), ())), preferred_element_type=jnp.float32)


def dot_nn(x, w):
    return lax.dot_general(x, w, (((1,), (0,)), ((), ())), preferred_element_type=jnp.float32)


def spread(tile, half, lanes_half):
    wide = tile.astype(jnp.float32)
    width = wide.shape[1] // 2
    if half != lanes_half:
        wide = pltpu.roll(wide, width, 1)
    lane = lax.broadcasted_iota(jnp.int32, wide.shape, 1)
    keep = lane < width if lanes_half == 0 else lane >= width
    return jnp.where(keep, wide, 0.0).astype(jnp.bfloat16)


def kernel(
    dims, src, leaf_in, transfer, leaf_out, out,
    src_v, in_v, tr_v, out_w_v, w_in, w_loc, w_own, w_par, w_out, held, got, res,
    src_sem, w_sem, out_sem, send_sem, recv_sem,
):
    local_bits, narrow_bits, wide_bits, blocks, rank, chunks, rows, halves = dims
    exchanges = narrow_bits + wide_bits
    cols = blocks * rank

    partners = []
    for axis, bits in (("narrow", narrow_bits), ("wide", wide_bits)):
        me = lax.axis_index(axis)
        for bit in range(bits):
            step = 1 << bit
            flag = lax.rem(lax.div(me, step), 2)
            partners.append({axis: me + step * (1 - 2 * flag)})

    barrier = pltpu.get_barrier_semaphore()
    for partner in partners:
        pl.semaphore_signal(barrier, inc=1, device_id=partner, device_id_type=MESH)

    def rows_of(c):
        return lax.rem(c, halves), pl.ds(pl.multiple_of(lax.div(c, halves) * rows, rows), rows)

    def src_copy(c):
        h, r = rows_of(c)
        return pltpu.make_async_copy(src.at[halves - 1 - h, r], src_v.at[c], src_sem.at[c])

    def out_copy(c):
        h, r = rows_of(c)
        return pltpu.make_async_copy(res.at[c], out.at[h, r], out_sem.at[c])

    in_copy = pltpu.make_async_copy(leaf_in, in_v, w_sem.at[0])
    loc_copy = pltpu.make_async_copy(transfer.at[pl.ds(0, local_bits)], tr_v.at[pl.ds(0, local_bits)], w_sem.at[1])
    ex_copy = pltpu.make_async_copy(transfer.at[pl.ds(local_bits, exchanges)], tr_v.at[pl.ds(local_bits, exchanges)], w_sem.at[2])
    last_copy = pltpu.make_async_copy(leaf_out, out_w_v, w_sem.at[3])
    in_copy.start()
    loc_copy.start()
    lax.fori_loop(0, chunks, lambda c, _: (src_copy(c).start(), None)[1], None)
    ex_copy.start()
    last_copy.start()

    def leaf_build(dst, leaf):
        dst[...] = jnp.zeros_like(dst)
        for h in range(halves):
            for k in range(blocks):
                w = leaf[h, k]
                tile = jnp.concatenate([w, w], axis=1)
                at = k * rank // (2 * rank) * 2 * rank
                dst[h, k * rank:(k + 1) * rank, at:at + 2 * rank] = spread(tile, k % 2, k % 2)

    in_copy.wait()
    leaf_build(w_in, in_v)
    loc_copy.wait()
    w_loc[...] = jnp.zeros_like(w_loc)
    for level in range(local_bits):
        for h in range(halves):
            for k in range(blocks):
                w = tr_v[level, h, k]
                p = k ^ (1 << level)
                r = slice(k * rank, (k + 1) * rank)
                own = spread(w, 0, k % 2)
                par = spread(w, 1, p % 2)
                ka, pa = k // 2 * 2 * rank, p // 2 * 2 * rank
                if ka == pa:
                    w_loc[level, h, r, ka:ka + 2 * rank] = own + par
                else:
                    w_loc[level, h, r, ka:ka + 2 * rank] = own
                    w_loc[level, h, r, pa:pa + 2 * rank] = par

    def send(e, c):
        return pltpu.make_async_remote_copy(
            src_ref=held.at[e, c],
            dst_ref=got.at[e, c],
            send_sem=send_sem.at[e, c],
            recv_sem=recv_sem.at[e, c],
            device_id=partners[e],
            device_id_type=MESH,
        )

    def first(c):
        h, _ = rows_of(c)
        src_copy(c).wait()
        x = dot_nn(src_v[c], w_in[h]).astype(jnp.bfloat16)
        for level in range(local_bits):
            x = dot_nt(x, w_loc[level, h]).astype(jnp.bfloat16)
        held[0, c] = x

    def mix(e, c):
        h, _ = rows_of(c)
        acc = dot_nt(held[e, c], w_own[e, h])
        send(e, c).wait_recv()
        acc = acc + dot_nt(got[e, c], w_par[e, h])
        x = acc.astype(jnp.bfloat16)
        if e + 1 < exchanges:
            held[e + 1, c] = x
            send(e + 1, c).start()
        else:
            res[c] = dot_nn(x, w_out[h]).astype(jnp.bfloat16)
            out_copy(c).start()

    gaps = list(FIRST_GAPS[:exchanges]) + [GAP] * (exchanges - len(FIRST_GAPS))
    after = [sum(gaps[:e + 1]) for e in range(exchanges)]
    lead = after[0]

    first(0)
    pl.semaphore_wait(barrier, len(partners))
    send(0, 0).start()

    def ahead(c, _):
        first(c)
        send(0, c).start()

    lax.fori_loop(1, lead, ahead, None)

    ex_copy.wait()
    w_own[...] = jnp.zeros_like(w_own)
    w_par[...] = jnp.zeros_like(w_par)
    for e in range(exchanges):
        for h in range(halves):
            for k in range(blocks):
                w = tr_v[local_bits + e, h, k]
                r = slice(k * rank, (k + 1) * rank)
                at = k // 2 * 2 * rank
                w_own[e, h, r, at:at + 2 * rank] = spread(w, 0, k % 2)
                w_par[e, h, r, at:at + 2 * rank] = spread(w, 1, k % 2)
    last_copy.wait()
    leaf_build(w_out, out_w_v)

    def step(t, _):
        for e in range(exchanges):
            c = t - after[e]
            if e == 1:
                @pl.when(t < chunks)
                def _():
                    first(t)
                    send(0, t).start()

            @pl.when((c >= 0) & (c < chunks))
            def _(e=e, c=c):
                mix(e, c)

    lax.fori_loop(lead, chunks + after[-1], step, None)

    def finish(c, _):
        out_copy(c).wait()
        for e in range(exchanges):
            send(e, c).wait_send()

    lax.fori_loop(0, chunks, finish, None)


def shards(sources, leaf_in, transfer, leaf_out):
    halves, points_rows, cols = sources.shape
    blocks, leaf, rank = leaf_in.shape[1:]
    levels = transfer.shape[0]
    local_bits = blocks.bit_length() - 1
    narrow_bits = lax.axis_size("narrow").bit_length() - 1
    wide_bits = lax.axis_size("wide").bit_length() - 1
    exchanges = narrow_bits + wide_bits
    rows = CHUNK_ROWS
    chunks = halves * points_rows // rows
    dims = (local_bits, narrow_bits, wide_bits, blocks, rank, chunks, rows, halves)
    bf = jnp.bfloat16
    any_spec = pl.BlockSpec(memory_space=pl.ANY)
    return pl.pallas_call(
        functools.partial(kernel, dims),
        out_shape=jax.ShapeDtypeStruct(sources.shape, bf),
        in_specs=[any_spec] * 4,
        out_specs=any_spec,
        scratch_shapes=[
            pltpu.VMEM((chunks, rows, cols), bf),
            pltpu.VMEM(leaf_in.shape, bf),
            pltpu.VMEM(transfer.shape, bf),
            pltpu.VMEM(leaf_out.shape, bf),
            pltpu.VMEM((halves, cols, cols), bf),
            pltpu.VMEM((local_bits, halves, cols, cols), bf),
            pltpu.VMEM((exchanges, halves, cols, cols), bf),
            pltpu.VMEM((exchanges, halves, cols, cols), bf),
            pltpu.VMEM((halves, cols, cols), bf),
            pltpu.VMEM((exchanges, chunks, rows, cols), bf),
            pltpu.VMEM((exchanges, chunks, rows, cols), bf),
            pltpu.VMEM((chunks, rows, cols), bf),
            pltpu.SemaphoreType.DMA((chunks,)),
            pltpu.SemaphoreType.DMA((4,)),
            pltpu.SemaphoreType.DMA((chunks,)),
            pltpu.SemaphoreType.DMA((exchanges, chunks)),
            pltpu.SemaphoreType.DMA((exchanges, chunks)),
        ],
        compiler_params=pltpu.CompilerParams(
            collective_id=0, has_side_effects=True, vmem_limit_bytes=60 * 1024 * 1024
        ),
    )(sources, leaf_in, transfer, leaf_out)


def solution(mesh):
    return jax.shard_map(
        shards,
        mesh=mesh,
        in_specs=(
            P(None, None, ("wide", "narrow")),
            P(None, ("wide", "narrow"), None, None),
            P(None, None, ("wide", "narrow"), None, None),
            P(None, ("wide", "narrow"), None, None),
        ),
        out_specs=P(None, None, ("wide", "narrow")),
        check_vma=False,
    )
```
